32 devices in a mesh: blk: 4 (over z), virt: 8 (over y, x, core).
Axes of the slice: x: 2, y: 2, z: 4, core: 2. Of those that a mesh axis runs over, the one named last changes fastest.
Arguments:
- integrals: bfloat16 [512, 16, 4096], P(('blk', 'virt')), may hold values from -0.09375 to 0.09375
- amplitudes: bfloat16 [256, 4096], P('blk'), may hold values from -6 to 6
- readers: int32 [512], P(('blk', 'virt')), may hold values from 0 to 7, as said below
- row_slots: int32 [512], P(('blk', 'virt')), may hold values from 0 to 3
- tile_mask: int32 [512, 4], P(('blk', 'virt')), may hold values 0 or 1
- virt_energy: float32 [2048], P(('blk', 'virt')), may hold values from 1 to 3
- occ_energy: float32 [1200], replicated, may hold values from -1 to -0.25
- pair_first: int32 [256], replicated, may hold values from 0 to 1199
- pair_second: int32 [256], replicated, may hold values from 0 to 1199
Outputs:
- update: bfloat16 [2048, 256], P(('blk', 'virt'))
The draws below stay inside these ranges and needn't reach their ends.
Inputs may be any that keep to these rules, and one draw needn't show every extreme that they name: `readers`: each tile names a reader on the virt axis in the same blk row as its generating device; one device names one reader at most 4 times, and in every blk row some reader is named 4 times by every device of that row.
All inputs are finite; a program needn't handle non-finite values. No bound on the sum of `tile_mask` on one device may be relied on, other than what follows from the above.
Results may differ from the reference program's by a relative error of at most 0.001.
Values may be sent and summed in bfloat16 or wider, within the bound.
A program may use at most 64 MiB of HBM per device.

```python
import jax
import jax.numpy as jnp
from jax import lax

TW = 4096
NOCC = 1200
TR = 16
GEN = 16
RB_DEV = 4
OPB = 64
TILES = 512
IJ = 256
ROWS = 2048
N_BLK = 4
N_VIRT = 8


def draw_readers(key, part):
    capacity = max(1, 2 * GEN // N_VIRT)
    slot_count = N_VIRT * capacity
    key_hot = jax.random.fold_in(key, 11)
    key_pref = jax.random.fold_in(key, 12)
    key_jitter = jax.random.fold_in(key, 13)
    hot_reader = jax.random.randint(key_hot, (N_BLK,), 0, N_VIRT)
    preference = jax.random.randint(key_pref, (N_BLK, N_VIRT), 0, 4)
    preference = jnp.where(jnp.arange(N_VIRT)[None, :] == hot_reader[:, None], 16, preference)
    device_pref = jnp.repeat(preference, N_VIRT, axis=0)
    slot_pref = jnp.repeat(device_pref, capacity, axis=1)
    jitter_values = jax.random.randint(key_jitter, (N_BLK * N_VIRT, slot_count), 0, 65536)
    scores = (slot_pref * 32768 + jitter_values) * slot_count + jnp.arange(slot_count)[None, :]
    ranking = jnp.argsort(-scores, axis=1)[:, :GEN]
    chosen = ranking // capacity
    return chosen.reshape(-1).astype(jnp.int32)


def touch_ends(entries, rng, least, top_value):
    shape = entries.shape
    place = [jax.random.randint(jax.random.fold_in(rng, axis), (), 0, shape[axis]) for axis in range(len(shape))]
    entries = entries.at[tuple(place)].set(least)
    longest = shape.index(max(shape))
    place[longest] = (place[longest] + 1) % shape[longest]
    return entries.at[tuple(place)].set(top_value)


def levels(key, extent, cuts, least, high):
    factor_of = 1.0
    for position, blocks in cuts:
        heights = jax.random.uniform(jax.random.fold_in(jax.random.fold_in(key, 6), position), (blocks,), jnp.float32, least / len(cuts), high / len(cuts))
        factor_of = factor_of * jnp.repeat(jnp.exp(heights), extent[position] // blocks).reshape((-1,) + (1,) * (len(extent) - 1 - position))
    return factor_of


def centred(own_key, extent, scale, reach, split=(), kind=jnp.bfloat16):
    drawn = scale * jax.random.normal(own_key, extent, jnp.float32)
    if split:
        drawn = drawn * levels(own_key, extent, split, -0.22, 0.18)
    return jnp.clip(drawn, -reach, reach).astype(kind)


def setup_inputs(seed: int = 0) -> dict:
    streams_of = jax.random.split(jax.random.key(seed), 10)
    integrals = centred(streams_of[0], (TILES, TR, TW), TW ** -0.5, 0.09375, ((0, 32),))
    amplitudes = centred(streams_of[1], (IJ, TW), 1.0, 6.0, ((0, 4),))
    readers = draw_readers(jax.random.fold_in(streams_of[9], 71), 0)
    row_slots = touch_ends(jax.random.randint(streams_of[3], (TILES,), 0, RB_DEV), jax.random.fold_in(streams_of[3], 1), 0, RB_DEV - 1).astype(jnp.int32)
    tile_mask = touch_ends((jax.random.randint(streams_of[4], (TILES, N_BLK), 0, 2) < 1).astype(jnp.int32), jax.random.fold_in(streams_of[4], 1), 0, 1)
    virt_energy = jnp.clip(1.0 + 2.0 * jax.random.uniform(streams_of[5], (ROWS,), jnp.float32) ** levels(streams_of[5], (ROWS,), ((0, 32),), -0.2, 0.2), 1.0, 3.0)
    occ_energy = jnp.clip(jax.random.uniform(streams_of[6], (NOCC,), jnp.float32, -1.0, -0.25), -1.0, -0.25)
    pair_first = touch_ends(jax.random.randint(streams_of[7], (IJ,), 0, NOCC), jax.random.fold_in(streams_of[7], 1), 0, NOCC - 1).astype(jnp.int32)
    pair_second = touch_ends(jax.random.randint(streams_of[8], (IJ,), 0, NOCC), jax.random.fold_in(streams_of[8], 1), 0, NOCC - 1).astype(jnp.int32)
    return dict(integrals=integrals, amplitudes=amplitudes, readers=readers, row_slots=row_slots, tile_mask=tile_mask, virt_energy=virt_energy, occ_energy=occ_energy, pair_first=pair_first, pair_second=pair_second)


def reference(integrals, amplitudes, readers, row_slots, tile_mask, virt_energy, occ_energy, pair_first, pair_second):
    devices = N_BLK * N_VIRT
    rows_dev = RB_DEV * TR
    amps_float = amplitudes.astype(jnp.float32)
    tile_array = integrals.reshape(devices, GEN, TR, TW)
    dest_all = readers.reshape(devices, GEN)
    slot_all = row_slots.reshape(devices, GEN)
    mask_all = tile_mask.reshape(devices, GEN, N_BLK)

    def accumulate(running, inputs):
        source, tile_block, dest_now, slot_now, mask_now = inputs
        product = jnp.einsum('gtw,pw->gtp', tile_block.astype(jnp.float32), amps_float,
                             precision=lax.Precision.HIGHEST)
        weight = jnp.repeat(mask_now.astype(jnp.float32), OPB, axis=1)
        product = product * weight[:, None, :]
        first_row = ((source // N_VIRT) * N_VIRT + dest_now) * rows_dev + slot_now * TR
        row_index = (first_row[:, None] + jnp.arange(TR, dtype=jnp.int32)[None, :]).astype(jnp.int32)
        running = running.at[row_index.reshape(-1)].add(product.reshape(GEN * TR, IJ))
        return running, None

    summed, _ = lax.scan(accumulate, jnp.zeros((ROWS, IJ), jnp.float32),
                         (jnp.arange(devices, dtype=jnp.int32), tile_array, dest_all, slot_all, mask_all))
    denominator = virt_energy[:, None] - occ_energy[pair_first][None, :] - occ_energy[pair_second][None, :]
    return (summed / denominator).astype(jnp.bfloat16)
```

```python
import functools

import jax
import jax.numpy as jnp
from jax import lax
from jax.experimental import pallas as pl
from jax.experimental.pallas import tpu as pltpu
from jax.sharding import PartitionSpec as P

MESH = pl.DeviceIdType.MESH


def flip(index, bits):
    step = 1
    while step <= bits:
        if bits & step:
            index = index + step * (1 - 2 * ((index // step) % 2))
        step *= 2
    return index


def kernel(
    blk_count,
    virt_count,
    tiles_hbm,
    amp_hbm,
    readers_hbm,
    slots_hbm,
    mask_hbm,
    virt_hbm,
    occ_hbm,
    first_hbm,
    second_hbm,
    out_ref,
    tiles,
    amp,
    partial,
    landed,
    denominator,
    hot,
    readers,
    slots,
    mask,
    virt_energy,
    occ,
    first,
    second,
    local_sem,
    z_send,
    z_recv,
    n_send,
    n_recv,
    sum_send,
    sum_recv,
):
    b = lax.axis_index("blk")
    v = lax.axis_index("virt")
    core = v % 2
    chip = v // 2
    kind = ((chip % 2) + ((chip // 2) % 2)) % 2
    generated = readers.shape[0]
    tile_rows = tiles.shape[0] // generated
    panel_rows, width = amp_hbm.shape
    rows = out_ref.shape[0]
    row_blocks = rows // tile_rows
    pairs = blk_count // 2

    locals_ = [
        pltpu.make_async_copy(source, target, local_sem.at[index])
        for index, (source, target) in enumerate(
            (
                (readers_hbm, readers),
                (slots_hbm, slots),
                (mask_hbm, mask),
                (virt_hbm, virt_energy),
                (occ_hbm, occ),
                (first_hbm, first),
                (second_hbm, second),
                (amp_hbm, amp.at[pl.ds(b * panel_rows, panel_rows)]),
                (tiles_hbm, tiles),
            )
        )
    ]

    barrier = pltpu.get_barrier_semaphore()
    for d in range(1, blk_count):
        pl.semaphore_signal(barrier, inc=1, device_id=(flip(b, d), v), device_id_type=MESH)
    for d in range(1, virt_count):
        pl.semaphore_signal(barrier, inc=1, device_id=(b, flip(v, d)), device_id_type=MESH)
    for copy in locals_:
        copy.start()
    pl.semaphore_wait(barrier, blk_count + virt_count - 2)

    half, quarter, eighth = width // 2, width // 4, width // 8

    def columns(core_now, kind_now):
        return pl.multiple_of(core_now * half + kind_now * quarter, quarter)

    def panel(d):
        return pl.ds(pl.multiple_of(flip(b, d) * panel_rows, panel_rows), panel_rows)

    mine = columns(core, kind)
    across = columns(core, 1 - kind)

    z_copies = {}
    for d in range(1, blk_count):
        copy = pltpu.make_async_remote_copy(
            amp_hbm.at[:, pl.ds(mine, quarter)],
            amp.at[panel(0), pl.ds(mine, quarter)],
            z_send.at[d],
            z_recv.at[d],
            device_id=(flip(b, d), v),
            device_id_type=MESH,
        )
        copy.start()
        z_copies[d] = copy

    n_copies = {}

    def share(d, which, start, size, bits):
        area = amp.at[panel(d), pl.ds(start, size)]
        copy = pltpu.make_async_remote_copy(
            area,
            area,
            n_send.at[d, which],
            n_recv.at[d, which],
            device_id=(b, flip(v, bits)),
            device_id_type=MESH,
        )
        copy.start()
        n_copies[d, which] = copy

    def spread(d):
        z_copies[d].wait_recv()
        share(d, 0, mine, eighth, 2)
        share(d, 1, pl.multiple_of(mine + eighth, eighth), eighth, 4)
        share(d, 2, mine, quarter, 1)

    def forward(d):
        n_copies[d, 0].wait_recv()
        n_copies[d, 1].wait_recv()
        share(d, 3, across, quarter, 1)

    def settle(d):
        n_copies[d, 2].wait_recv()
        n_copies[d, 3].wait_recv()

    for copy in locals_[:7]:
        copy.wait()
    all_rows = virt_count * rows
    lanes = generated * tile_rows
    lane = lax.broadcasted_iota(jnp.int32, (1, lanes), 1)
    goal = jnp.zeros((1, lanes), jnp.int32)
    for t in range(generated):
        goal = jnp.where(
            lane // tile_rows == t, (readers[t] * row_blocks + slots[t]) * tile_rows, goal
        )
    goal = goal + lane % tile_rows
    row = lax.broadcasted_iota(jnp.int32, (all_rows, lanes), 0)
    hot[...] = (row == goal).astype(jnp.float32).astype(jnp.bfloat16)

    levels = occ.shape[1]
    occ_high = occ[...].astype(jnp.bfloat16).astype(jnp.float32)
    occ_rest = occ[...] - occ_high
    occ_mid = occ_rest.astype(jnp.bfloat16).astype(jnp.float32)
    occ_low = occ_rest - occ_mid
    term = lax.broadcasted_iota(jnp.int32, (8, levels), 0)
    occ_terms = jnp.where(
        term == 0, occ_high, jnp.where(term == 1, occ_mid, jnp.where(term == 2, occ_low, 0.0))
    ).astype(jnp.bfloat16)
    count = first.shape[1]
    level = lax.broadcasted_iota(jnp.int32, (levels, count), 0)

    def energy(pair_ref):
        chosen = (level == pair_ref[...]).astype(jnp.float32).astype(jnp.bfloat16)
        terms = jnp.dot(occ_terms, chosen, preferred_element_type=jnp.float32)
        return (terms[0:1] + terms[1:2]) + terms[2:3]

    diagonal = lax.broadcasted_iota(jnp.int32, (rows, rows), 0) == lax.broadcasted_iota(
        jnp.int32, (rows, rows), 1
    )
    virt_column = jnp.sum(jnp.where(diagonal, virt_energy[...], 0.0), axis=1, keepdims=True)
    denominator[...] = (virt_column - energy(first)) - energy(second)

    sums = {}
    pair_width = 2 * panel_rows
    pair_lane = lax.broadcasted_iota(jnp.int32, (1, pair_width), 1)

    def contract(i):
        g = flip(b // 2, i)
        block = amp[pl.ds(pl.multiple_of(g * pair_width, pair_width), pair_width), :]
        product = lax.dot_general(
            tiles[...], block, (((1,), (1,)), ((), ())), preferred_element_type=jnp.float32
        )
        weight = jnp.concatenate(
            [
                jnp.broadcast_to(
                    jnp.where(pair_lane < panel_rows, mask[t, 2 * g], mask[t, 2 * g + 1]).astype(
                        jnp.float32
                    ),
                    (tile_rows, pair_width),
                )
                for t in range(generated)
            ],
            axis=0,
        )
        product = product * weight
        high = product.astype(jnp.bfloat16)
        low = (product - high.astype(jnp.float32)).astype(jnp.bfloat16)
        partial[i] = jnp.dot(hot[...], high, preferred_element_type=jnp.float32) + jnp.dot(
            hot[...], low, preferred_element_type=jnp.float32
        )
        for d in range(1, virt_count):
            peer = flip(v, d)
            copy = pltpu.make_async_remote_copy(
                partial.at[i, pl.ds(pl.multiple_of(peer * rows, rows), rows)],
                landed.at[i, d],
                sum_send.at[i, d],
                sum_recv.at[i, d],
                device_id=(b, peer),
                device_id_type=MESH,
            )
            copy.start()
            sums[i, d] = copy

    spread(1)
    forward(1)
    settle(1)
    locals_[7].wait()
    locals_[8].wait()
    contract(0)
    for i in range(1, pairs):
        spread(2 * i)
        spread(2 * i + 1)
        forward(2 * i)
        forward(2 * i + 1)
        settle(2 * i)
        settle(2 * i + 1)
        contract(i)

    for i in range(pairs):
        start = pl.multiple_of(flip(b // 2, i) * pair_width, pair_width)
        total = partial[i, pl.ds(pl.multiple_of(v * rows, rows), rows), :]
        for d in range(1, virt_count):
            sums[i, d].wait_recv()
            total = total + landed[i, d]
        out_ref[:, pl.ds(start, pair_width)] = (
            total / denominator[:, pl.ds(start, pair_width)]
        ).astype(out_ref.dtype)

    for copies in (z_copies, n_copies, sums):
        for copy in copies.values():
            copy.wait_send()


def body(
    blk_count,
    virt_count,
    integrals,
    amplitudes,
    readers,
    row_slots,
    tile_mask,
    virt_energy,
    occ_energy,
    pair_first,
    pair_second,
):
    generated, tile_rows, width = integrals.shape
    panel_rows = amplitudes.shape[0]
    rows = virt_energy.shape[0]
    columns = blk_count * panel_rows
    pairs = blk_count // 2
    levels = occ_energy.shape[0]
    anywhere = pl.BlockSpec(memory_space=pl.ANY)
    return pl.pallas_call(
        functools.partial(kernel, blk_count, virt_count),
        out_shape=jax.ShapeDtypeStruct((rows, columns), jnp.bfloat16),
        in_specs=[anywhere] * 9,
        out_specs=pl.BlockSpec(memory_space=pltpu.VMEM),
        scratch_shapes=[
            pltpu.VMEM((generated * tile_rows, width), jnp.bfloat16),
            pltpu.VMEM((columns, width), jnp.bfloat16),
            pltpu.VMEM((pairs, virt_count * rows, 2 * panel_rows), jnp.float32),
            pltpu.VMEM((pairs, virt_count, rows, 2 * panel_rows), jnp.float32),
            pltpu.VMEM((rows, columns), jnp.float32),
            pltpu.VMEM((virt_count * rows, generated * tile_rows), jnp.bfloat16),
            pltpu.SMEM((generated,), jnp.int32),
            pltpu.SMEM((generated,), jnp.int32),
            pltpu.SMEM((generated, blk_count), jnp.int32),
            pltpu.VMEM((1, rows), jnp.float32),
            pltpu.VMEM((1, levels), jnp.float32),
            pltpu.VMEM((1, columns), jnp.int32),
            pltpu.VMEM((1, columns), jnp.int32),
            pltpu.SemaphoreType.DMA((9,)),
            pltpu.SemaphoreType.DMA((blk_count,)),
            pltpu.SemaphoreType.DMA((blk_count,)),
            pltpu.SemaphoreType.DMA((blk_count, 4)),
            pltpu.SemaphoreType.DMA((blk_count, 4)),
            pltpu.SemaphoreType.DMA((pairs, virt_count)),
            pltpu.SemaphoreType.DMA((pairs, virt_count)),
        ],
        compiler_params=pltpu.CompilerParams(
            collective_id=0, has_side_effects=True, vmem_limit_bytes=48 * 1024 * 1024
        ),
        name="ladder",
    )(
        integrals.reshape(generated * tile_rows, width),
        amplitudes,
        readers,
        row_slots,
        tile_mask,
        virt_energy.reshape(1, rows),
        occ_energy.reshape(1, levels),
        pair_first.reshape(1, columns),
        pair_second.reshape(1, columns),
    )


def solution(mesh):
    placed = (
        P(("blk", "virt"), None, None),
        P("blk", None),
        P(("blk", "virt")),
        P(("blk", "virt")),
        P(("blk", "virt"), None),
        P(("blk", "virt")),
        P(),
        P(),
        P(),
    )
    return jax.shard_map(
        functools.partial(body, mesh.shape["blk"], mesh.shape["virt"]),
        mesh=mesh,
        in_specs=placed,
        out_specs=P(("blk", "virt"), None),
        check_vma=False,
    )
```

```python
import functools

import jax
import jax.numpy as jnp
from jax import lax
from jax.experimental import pallas as pl
from jax.experimental.pallas import tpu as pltpu
from jax.sharding import PartitionSpec as P

MESH = pl.DeviceIdType.MESH


def flip(index, bits):
    step = 1
    while step <= bits:
        if bits & step:
            index = index + step * (1 - 2 * ((index // step) % 2))
        step *= 2
    return index


def kernel(
    blk_count,
    virt_count,
    tiles_hbm,
    amp_hbm,
    readers_hbm,
    slots_hbm,
    mask_hbm,
    virt_hbm,
    occ_hbm,
    first_hbm,
    second_hbm,
    out_ref,
    tiles,
    amp,
    partial,
    swapped,
    landed,
    denominator,
    hot,
    readers,
    slots,
    mask,
    virt_energy,
    occ,
    first,
    second,
    local_sem,
    z_send,
    z_recv,
    n_send,
    n_recv,
    sum_send,
    sum_recv,
):
    b = lax.axis_index("blk")
    v = lax.axis_index("virt")
    core = v % 2
    chip = v // 2
    kind = ((chip % 2) + ((chip // 2) % 2)) % 2
    generated = readers.shape[0]
    tile_rows = tiles.shape[0] // generated
    panel_rows, width = amp_hbm.shape
    rows = out_ref.shape[0]
    row_blocks = rows // tile_rows
    pairs = blk_count // 2

    locals_ = [
        pltpu.make_async_copy(source, target, local_sem.at[index])
        for index, (source, target) in enumerate(
            (
                (readers_hbm, readers),
                (slots_hbm, slots),
                (mask_hbm, mask),
                (virt_hbm, virt_energy),
                (occ_hbm, occ),
                (first_hbm, first),
                (second_hbm, second),
                (amp_hbm, amp.at[pl.ds(b * panel_rows, panel_rows)]),
                (tiles_hbm, tiles),
            )
        )
    ]

    barrier = pltpu.get_barrier_semaphore()
    for d in range(1, blk_count):
        pl.semaphore_signal(barrier, inc=1, device_id=(flip(b, d), v), device_id_type=MESH)
    for d in range(1, virt_count):
        pl.semaphore_signal(barrier, inc=1, device_id=(b, flip(v, d)), device_id_type=MESH)
    for copy in locals_:
        copy.start()
    pl.semaphore_wait(barrier, blk_count + virt_count - 2)

    half, piece = width // 2, width // 8
    spot = chip % 4

    def columns(core_now, spot_now):
        return pl.multiple_of(core_now * half + spot_now * piece, piece)

    def panel(d):
        return pl.ds(pl.multiple_of(flip(b, d) * panel_rows, panel_rows), panel_rows)

    mine = columns(core, spot)
    beside_x = columns(core, flip(spot, 1))
    beside_y = columns(core, flip(spot, 2))
    opposite = columns(core, flip(spot, 3))

    z_copies = {}
    for d in range(1, blk_count):
        copy = pltpu.make_async_remote_copy(
            amp_hbm.at[:, pl.ds(mine, piece)],
            amp.at[panel(0), pl.ds(mine, piece)],
            z_send.at[d],
            z_recv.at[d],
            device_id=(flip(b, d), v),
            device_id_type=MESH,
        )
        copy.start()
        z_copies[d] = copy

    n_copies = {}

    def share(d, which, start, size, bits):
        area = amp.at[panel(d), pl.ds(start, size)]
        copy = pltpu.make_async_remote_copy(
            area,
            area,
            n_send.at[d, which],
            n_recv.at[d, which],
            device_id=(b, flip(v, bits)),
            device_id_type=MESH,
        )
        copy.start()
        n_copies[d, which] = copy

    def spread(d):
        z_copies[d].wait_recv()
        share(d, 0, mine, piece, 2)
        share(d, 1, mine, piece, 4)
        share(d, 2, mine, piece, 1)

    def relay(d):
        n_copies[d, 0].wait_recv()
        share(d, 3, beside_x, piece // 2, 4)
        n_copies[d, 1].wait_recv()
        share(d, 4, pl.multiple_of(beside_y + piece // 2, piece // 2), piece // 2, 2)
        share(d, 5, beside_x, piece, 1)
        share(d, 6, beside_y, piece, 1)

    def finish(d):
        n_copies[d, 3].wait_recv()
        n_copies[d, 4].wait_recv()
        share(d, 7, opposite, piece, 1)

    def settle(d):
        for which in (2, 5, 6, 7):
            n_copies[d, which].wait_recv()

    for copy in locals_[:7]:
        copy.wait()
    chips = virt_count // 2
    all_rows = virt_count * rows
    core_rows = chips * rows
    lanes = generated * tile_rows
    lane = lax.broadcasted_iota(jnp.int32, (1, lanes), 1)
    goal = jnp.zeros((1, lanes), jnp.int32)
    for t in range(generated):
        place = (readers[t] % 2) * chips + readers[t] // 2
        goal = jnp.where(lane // tile_rows == t, (place * row_blocks + slots[t]) * tile_rows, goal)
    goal = goal + lane % tile_rows
    row = lax.broadcasted_iota(jnp.int32, (all_rows, lanes), 0)
    hot[...] = (row == goal).astype(jnp.float32).astype(jnp.bfloat16)

    levels = occ.shape[0]
    occ_row = occ[...].reshape(1, levels)
    occ_high = occ_row.astype(jnp.bfloat16).astype(jnp.float32)
    occ_rest = occ_row - occ_high
    occ_mid = occ_rest.astype(jnp.bfloat16).astype(jnp.float32)
    occ_low = occ_rest - occ_mid
    term = lax.broadcasted_iota(jnp.int32, (8, levels), 0)
    occ_terms = jnp.where(
        term == 0, occ_high, jnp.where(term == 1, occ_mid, jnp.where(term == 2, occ_low, 0.0))
    ).astype(jnp.bfloat16)
    count = first.shape[1]
    level = lax.broadcasted_iota(jnp.int32, (levels, count), 0)

    def energy(pair_ref):
        chosen = (level == pair_ref[...]).astype(jnp.float32).astype(jnp.bfloat16)
        terms = jnp.dot(occ_terms, chosen, preferred_element_type=jnp.float32)
        return (terms[0:1] + terms[1:2]) + terms[2:3]

    diagonal = lax.broadcasted_iota(jnp.int32, (rows, rows), 0) == lax.broadcasted_iota(
        jnp.int32, (rows, rows), 1
    )
    virt_column = jnp.sum(jnp.where(diagonal, virt_energy[...], 0.0), axis=1, keepdims=True)
    denominator[...] = (virt_column - energy(first)) - energy(second)

    sums = {}
    pair_width = 2 * panel_rows
    pair_lane = lax.broadcasted_iota(jnp.int32, (1, pair_width), 1)

    def contract(i):
        g = flip(b // 2, i)
        block = amp[pl.ds(pl.multiple_of(g * pair_width, pair_width), pair_width), :]
        product = lax.dot_general(
            tiles[...], block, (((1,), (1,)), ((), ())), preferred_element_type=jnp.float32
        )
        weight = jnp.concatenate(
            [
                jnp.broadcast_to(
                    jnp.where(pair_lane < panel_rows, mask[2 * g, t], mask[2 * g + 1, t]).astype(
                        jnp.float32
                    ),
                    (tile_rows, pair_width),
                )
                for t in range(generated)
            ],
            axis=0,
        )
        product = product * weight
        high = product.astype(jnp.bfloat16)
        low = (product - high.astype(jnp.float32)).astype(jnp.bfloat16)
        partial[i] = jnp.dot(hot[...], high, preferred_element_type=jnp.float32) + jnp.dot(
            hot[...], low, preferred_element_type=jnp.float32
        )
        copy = pltpu.make_async_remote_copy(
            partial.at[i, pl.ds(pl.multiple_of((1 - core) * core_rows, core_rows), core_rows)],
            swapped.at[i],
            sum_send.at[i, 0],
            sum_recv.at[i, 0],
            device_id=(b, flip(v, 1)),
            device_id_type=MESH,
        )
        copy.start()
        sums[i, 0] = copy

    def scatter(i):
        own = pl.ds(pl.multiple_of(core * core_rows, core_rows), core_rows)
        sums[i, 0].wait_recv()
        swapped[i] = swapped[i] + partial[i, own, :]
        for d in range(1, chips):
            peer = flip(chip, d)
            copy = pltpu.make_async_remote_copy(
                swapped.at[i, pl.ds(pl.multiple_of(peer * rows, rows), rows)],
                landed.at[i, d],
                sum_send.at[i, d],
                sum_recv.at[i, d],
                device_id=(b, flip(v, 2 * d)),
                device_id_type=MESH,
            )
            copy.start()
            sums[i, d] = copy

    locals_[7].wait()
    locals_[8].wait()
    for i in range(1, pairs):
        if i == 1:
            spread(1)
        spread(2 * i)
        if i == 1:
            relay(1)
        spread(2 * i + 1)
        if i == 1:
            finish(1)
            settle(1)
        relay(2 * i)
        relay(2 * i + 1)
        if i == 1:
            contract(0)
            scatter(0)
        finish(2 * i)
        finish(2 * i + 1)
        settle(2 * i)
        settle(2 * i + 1)
        contract(i)
        scatter(i)

    for i in range(pairs):
        start = pl.multiple_of(flip(b // 2, i) * pair_width, pair_width)
        total = swapped[i, pl.ds(pl.multiple_of(chip * rows, rows), rows), :]
        for d in range(1, chips):
            sums[i, d].wait_recv()
            total = total + landed[i, d]
        out_ref[:, pl.ds(start, pair_width)] = (
            total / denominator[:, pl.ds(start, pair_width)]
        ).astype(out_ref.dtype)

    for copies in (z_copies, n_copies, sums):
        for copy in copies.values():
            copy.wait_send()


def body(
    blk_count,
    virt_count,
    integrals,
    amplitudes,
    readers,
    row_slots,
    tile_mask,
    virt_energy,
    occ_energy,
    pair_first,
    pair_second,
):
    generated, tile_rows, width = integrals.shape
    panel_rows = amplitudes.shape[0]
    rows = virt_energy.shape[0]
    columns = blk_count * panel_rows
    pairs = blk_count // 2
    levels = occ_energy.shape[0]
    anywhere = pl.BlockSpec(memory_space=pl.ANY)
    return pl.pallas_call(
        functools.partial(kernel, blk_count, virt_count),
        out_shape=jax.ShapeDtypeStruct((rows, columns), jnp.bfloat16),
        in_specs=[anywhere] * 9,
        out_specs=pl.BlockSpec(memory_space=pltpu.VMEM),
        scratch_shapes=[
            pltpu.VMEM((generated * tile_rows, width), jnp.bfloat16),
            pltpu.VMEM((columns, width), jnp.bfloat16),
            pltpu.VMEM((pairs, virt_count * rows, 2 * panel_rows), jnp.float32),
            pltpu.VMEM((pairs, virt_count // 2 * rows, 2 * panel_rows), jnp.float32),
            pltpu.VMEM((pairs, virt_count // 2, rows, 2 * panel_rows), jnp.float32),
            pltpu.VMEM((rows, columns), jnp.float32),
            pltpu.VMEM((virt_count * rows, generated * tile_rows), jnp.bfloat16),
            pltpu.SMEM((generated,), jnp.int32),
            pltpu.SMEM((generated,), jnp.int32),
            pltpu.SMEM((blk_count, generated), jnp.int32),
            pltpu.VMEM((1, rows), jnp.float32),
            pltpu.VMEM((levels,), jnp.float32),
            pltpu.VMEM((1, columns), jnp.int32),
            pltpu.VMEM((1, columns), jnp.int32),
            pltpu.SemaphoreType.DMA((9,)),
            pltpu.SemaphoreType.DMA((blk_count,)),
            pltpu.SemaphoreType.DMA((blk_count,)),
            pltpu.SemaphoreType.DMA((blk_count, 8)),
            pltpu.SemaphoreType.DMA((blk_count, 8)),
            pltpu.SemaphoreType.DMA((pairs, virt_count // 2)),
            pltpu.SemaphoreType.DMA((pairs, virt_count // 2)),
        ],
        compiler_params=pltpu.CompilerParams(
            collective_id=0, has_side_effects=True, vmem_limit_bytes=60 * 1024 * 1024
        ),
        name="ladder",
    )(
        integrals.reshape(generated * tile_rows, width),
        amplitudes,
        readers,
        row_slots,
        tile_mask.T,
        virt_energy.reshape(1, rows),
        occ_energy,
        pair_first.reshape(1, columns),
        pair_second.reshape(1, columns),
    )


def solution(mesh):
    placed = (
        P(("blk", "virt"), None, None),
        P("blk", None),
        P(("blk", "virt")),
        P(("blk", "virt")),
        P(("blk", "virt"), None),
        P(("blk", "virt")),
        P(),
        P(),
        P(),
    )
    return jax.shard_map(
        functools.partial(body, mesh.shape["blk"], mesh.shape["virt"]),
        mesh=mesh,
        in_specs=placed,
        out_specs=P(("blk", "virt"), None),
        check_vma=False,
    )
```

```python
import functools

import jax
import jax.numpy as jnp
from jax import lax
from jax.experimental import pallas as pl
from jax.experimental.pallas import tpu as pltpu
from jax.sharding import PartitionSpec as P

MESH = pl.DeviceIdType.MESH


def flip(index, bits):
    step = 1
    while step <= bits:
        if bits & step:
            index = index + step * (1 - 2 * ((index // step) % 2))
        step *= 2
    return index


def kernel(
    blk_count,
    virt_count,
    tiles_hbm,
    amp_hbm,
    readers_hbm,
    slots_hbm,
    mask_hbm,
    virt_hbm,
    occ_hbm,
    first_hbm,
    second_hbm,
    out_ref,
    tiles,
    amp,
    products,
    weights,
    partial,
    swapped,
    landed,
    denominator,
    hot,
    readers,
    slots,
    mask,
    virt_energy,
    occ,
    first,
    second,
    local_sem,
    z_send,
    z_recv,
    n_send,
    n_recv,
    sum_send,
    sum_recv,
):
    b = lax.axis_index("blk")
    v = lax.axis_index("virt")
    core = v % 2
    chip = v // 2
    kind = ((chip % 2) + ((chip // 2) % 2)) % 2
    generated = readers.shape[0]
    tile_rows = tiles.shape[0] // generated
    panel_rows, width = amp_hbm.shape
    rows = out_ref.shape[0]
    row_blocks = rows // tile_rows
    pairs = blk_count // 2

    locals_ = [
        pltpu.make_async_copy(source, target, local_sem.at[index])
        for index, (source, target) in enumerate(
            (
                (readers_hbm, readers),
                (slots_hbm, slots),
                (mask_hbm, mask),
                (virt_hbm, virt_energy),
                (occ_hbm, occ),
                (first_hbm, first),
                (second_hbm, second),
                (amp_hbm, amp.at[pl.ds(b * panel_rows, panel_rows)]),
                (tiles_hbm, tiles),
            )
        )
    ]

    barrier = pltpu.get_barrier_semaphore()
    for d in range(1, blk_count):
        pl.semaphore_signal(barrier, inc=1, device_id=(flip(b, d), v), device_id_type=MESH)
    for d in range(1, virt_count):
        pl.semaphore_signal(barrier, inc=1, device_id=(b, flip(v, d)), device_id_type=MESH)
    for copy in locals_:
        copy.start()
    pl.semaphore_wait(barrier, blk_count + virt_count - 2)

    half, piece = width // 2, width // 8
    spot = chip % 4

    def columns(core_now, spot_now):
        return pl.multiple_of(core_now * half + spot_now * piece, piece)

    def panel(d):
        return pl.ds(pl.multiple_of(flip(b, d) * panel_rows, panel_rows), panel_rows)

    mine = columns(core, spot)
    beside_x = columns(core, flip(spot, 1))
    beside_y = columns(core, flip(spot, 2))
    opposite = columns(core, flip(spot, 3))

    z_copies = {}
    for d in range(1, blk_count):
        copy = pltpu.make_async_remote_copy(
            amp_hbm.at[:, pl.ds(mine, piece)],
            amp.at[panel(0), pl.ds(mine, piece)],
            z_send.at[d],
            z_recv.at[d],
            device_id=(flip(b, d), v),
            device_id_type=MESH,
        )
        copy.start()
        z_copies[d] = copy

    n_copies = {}

    def share(d, which, start, size, bits):
        area = amp.at[panel(d), pl.ds(start, size)]
        copy = pltpu.make_async_remote_copy(
            area,
            area,
            n_send.at[d, which],
            n_recv.at[d, which],
            device_id=(b, flip(v, bits)),
            device_id_type=MESH,
        )
        copy.start()
        n_copies[d, which] = copy

    def spread(d):
        z_copies[d].wait_recv()
        share(d, 0, mine, piece, 2)
        share(d, 1, mine, piece, 4)
        if d == 1:
            share(d, 3, mine, piece, 6)
        share(d, 2, mine, piece, 1)

    def relay(d):
        n_copies[d, 0].wait_recv()
        if not d == 1:
            share(d, 3, beside_x, piece // 2, 4)
        n_copies[d, 1].wait_recv()
        if not d == 1:
            share(d, 4, pl.multiple_of(beside_y + piece // 2, piece // 2), piece // 2, 2)
        share(d, 5, beside_x, piece, 1)
        share(d, 6, beside_y, piece, 1)

    def finish(d):
        n_copies[d, 3].wait_recv()
        if not d == 1:
            n_copies[d, 4].wait_recv()
        share(d, 7, opposite, piece, 1)

    def settle(which, *panels):
        for d in panels:
            n_copies[d, which].wait_recv()

    for copy in locals_[:7]:
        copy.wait()
    chips = virt_count // 2
    all_rows = virt_count * rows
    core_rows = chips * rows
    lanes = generated * tile_rows
    lane = lax.broadcasted_iota(jnp.int32, (1, lanes), 1)
    goal = jnp.zeros((1, lanes), jnp.int32)
    for t in range(generated):
        place = (readers[t] % 2) * chips + readers[t] // 2
        goal = jnp.where(lane // tile_rows == t, (place * row_blocks + slots[t]) * tile_rows, goal)
    goal = goal + lane % tile_rows
    row = lax.broadcasted_iota(jnp.int32, (all_rows, lanes), 0)
    hot[...] = (row == goal).astype(jnp.float32).astype(jnp.bfloat16)

    levels = occ.shape[0]
    occ_row = occ[...].reshape(1, levels)
    occ_high = occ_row.astype(jnp.bfloat16).astype(jnp.float32)
    occ_rest = occ_row - occ_high
    occ_mid = occ_rest.astype(jnp.bfloat16).astype(jnp.float32)
    occ_low = occ_rest - occ_mid
    term = lax.broadcasted_iota(jnp.int32, (8, levels), 0)
    occ_terms = jnp.where(
        term == 0, occ_high, jnp.where(term == 1, occ_mid, jnp.where(term == 2, occ_low, 0.0))
    ).astype(jnp.bfloat16)
    count = first.shape[1]
    level = lax.broadcasted_iota(jnp.int32, (levels, count), 0)

    def energy(pair_ref):
        chosen = (level == pair_ref[...]).astype(jnp.float32).astype(jnp.bfloat16)
        terms = jnp.dot(occ_terms, chosen, preferred_element_type=jnp.float32)
        return (terms[0:1] + terms[1:2]) + terms[2:3]

    diagonal = lax.broadcasted_iota(jnp.int32, (rows, rows), 0) == lax.broadcasted_iota(
        jnp.int32, (rows, rows), 1
    )
    virt_column = jnp.sum(jnp.where(diagonal, virt_energy[...], 0.0), axis=1, keepdims=True)
    denominator[...] = (virt_column - energy(first)) - energy(second)

    sums = {}
    pair_width = 2 * panel_rows
    pair_lane = lax.broadcasted_iota(jnp.int32, (1, pair_width), 1)

    def multiply(i, spot_now, begin=False):
        rows_now = pl.ds(pl.multiple_of(flip(b // 2, i) * pair_width, pair_width), pair_width)
        total = None if begin else products[i]
        for core_now in range(2):
            depth = pl.ds(columns(core_now, spot_now), piece)
            term = lax.dot_general(
                tiles[:, depth],
                amp[rows_now, depth],
                (((1,), (1,)), ((), ())),
                preferred_element_type=jnp.float32,
            )
            total = term if total is None else total + term
        products[i] = total

    for i in range(pairs):
        g = flip(b // 2, i)
        weights[i] = jnp.concatenate(
            [
                jnp.broadcast_to(
                    jnp.where(pair_lane < panel_rows, mask[2 * g, t], mask[2 * g + 1, t]).astype(
                        jnp.float32
                    ),
                    (tile_rows, pair_width),
                )
                for t in range(generated)
            ],
            axis=0,
        )

    def contract(i):
        product = products[i]
        product = product * weights[i]
        high = product.astype(jnp.bfloat16)
        low = (product - high.astype(jnp.float32)).astype(jnp.bfloat16)
        terms = jnp.concatenate([high, low], axis=1)

        def gather_rows(core_now):
            area = pl.ds(pl.multiple_of(core_now * core_rows, core_rows), core_rows)
            both = jnp.dot(hot[area, :], terms, preferred_element_type=jnp.float32)
            partial[i, area, :] = both[:, :pair_width] + both[:, pair_width:]

        gather_rows(1 - core)
        copy = pltpu.make_async_remote_copy(
            partial.at[i, pl.ds(pl.multiple_of((1 - core) * core_rows, core_rows), core_rows)],
            swapped.at[i],
            sum_send.at[i, 0],
            sum_recv.at[i, 0],
            device_id=(b, flip(v, 1)),
            device_id_type=MESH,
        )
        copy.start()
        sums[i, 0] = copy
        gather_rows(core)

    def scatter(i):
        sums[i, 0].wait_recv()
        for d in (3, 1, 2) + tuple(range(4, chips)) + (0,):
            peer = flip(chip, d)
            area = pl.ds(pl.multiple_of(peer * rows, rows), rows)
            own = pl.ds(pl.multiple_of(core * core_rows + peer * rows, rows), rows)
            swapped[i, area, :] = swapped[i, area, :] + partial[i, own, :]
            if d == 0:
                continue
            copy = pltpu.make_async_remote_copy(
                swapped.at[i, area],
                landed.at[i, d],
                sum_send.at[i, d],
                sum_recv.at[i, d],
                device_id=(b, flip(v, 2 * d)),
                device_id_type=MESH,
            )
            copy.start()
            sums[i, d] = copy

    locals_[7].wait()
    locals_[8].wait()

    def gathered(i, step, *panels):
        settle((2, 5, 6, 7)[step], *panels)
        multiply(i, flip(spot, step), step == 0)

    for i in range(1, pairs):
        even, odd = 2 * i, 2 * i + 1
        if i == 1:
            spread(1)
        spread(even)
        spread(odd)
        if i == 1:
            relay(1)
            finish(1)
            for step in range(3):
                gathered(0, step, 1)
        relay(even)
        relay(odd)
        if i == 1:
            gathered(0, 3, 1)
            contract(0)
            scatter(0)
        for step in range(3):
            gathered(i, step, even, odd)
        finish(even)
        finish(odd)
        gathered(i, 3, even, odd)
        contract(i)
        scatter(i)

    for i in range(pairs):
        start = pl.multiple_of(flip(b // 2, i) * pair_width, pair_width)
        total = swapped[i, pl.ds(pl.multiple_of(chip * rows, rows), rows), :]
        for d in range(1, chips):
            sums[i, d].wait_recv()
            total = total + landed[i, d]
        out_ref[:, pl.ds(start, pair_width)] = (
            total / denominator[:, pl.ds(start, pair_width)]
        ).astype(out_ref.dtype)

    for copies in (z_copies, n_copies, sums):
        for copy in copies.values():
            copy.wait_send()


def body(
    blk_count,
    virt_count,
    integrals,
    amplitudes,
    readers,
    row_slots,
    tile_mask,
    virt_energy,
    occ_energy,
    pair_first,
    pair_second,
):
    generated, tile_rows, width = integrals.shape
    panel_rows = amplitudes.shape[0]
    rows = virt_energy.shape[0]
    columns = blk_count * panel_rows
    pairs = blk_count // 2
    levels = occ_energy.shape[0]
    anywhere = pl.BlockSpec(memory_space=pl.ANY)
    return pl.pallas_call(
        functools.partial(kernel, blk_count, virt_count),
        out_shape=jax.ShapeDtypeStruct((rows, columns), jnp.bfloat16),
        in_specs=[anywhere] * 9,
        out_specs=pl.BlockSpec(memory_space=pltpu.VMEM),
        scratch_shapes=[
            pltpu.VMEM((generated * tile_rows, width), jnp.bfloat16),
            pltpu.VMEM((columns, width), jnp.bfloat16),
            pltpu.VMEM((pairs, generated * tile_rows, 2 * panel_rows), jnp.float32),
            pltpu.VMEM((pairs, generated * tile_rows, 2 * panel_rows), jnp.float32),
            pltpu.VMEM((pairs, virt_count * rows, 2 * panel_rows), jnp.float32),
            pltpu.VMEM((pairs, virt_count // 2 * rows, 2 * panel_rows), jnp.float32),
            pltpu.VMEM((pairs, virt_count // 2, rows, 2 * panel_rows), jnp.float32),
            pltpu.VMEM((rows, columns), jnp.float32),
            pltpu.VMEM((virt_count * rows, generated * tile_rows), jnp.bfloat16),
            pltpu.SMEM((generated,), jnp.int32),
            pltpu.SMEM((generated,), jnp.int32),
            pltpu.SMEM((blk_count, generated), jnp.int32),
            pltpu.VMEM((1, rows), jnp.float32),
            pltpu.VMEM((levels,), jnp.float32),
            pltpu.VMEM((1, columns), jnp.int32),
            pltpu.VMEM((1, columns), jnp.int32),
            pltpu.SemaphoreType.DMA((9,)),
            pltpu.SemaphoreType.DMA((blk_count,)),
            pltpu.SemaphoreType.DMA((blk_count,)),
            pltpu.SemaphoreType.DMA((blk_count, 8)),
            pltpu.SemaphoreType.DMA((blk_count, 8)),
            pltpu.SemaphoreType.DMA((pairs, virt_count // 2)),
            pltpu.SemaphoreType.DMA((pairs, virt_count // 2)),
        ],
        compiler_params=pltpu.CompilerParams(
            collective_id=0, has_side_effects=True, vmem_limit_bytes=60 * 1024 * 1024
        ),
        name="ladder",
    )(
        integrals.reshape(generated * tile_rows, width),
        amplitudes,
        readers,
        row_slots,
        tile_mask.T,
        virt_energy.reshape(1, rows),
        occ_energy,
        pair_first.reshape(1, columns),
        pair_second.reshape(1, columns),
    )


def solution(mesh):
    placed = (
        P(("blk", "virt"), None, None),
        P("blk", None),
        P(("blk", "virt")),
        P(("blk", "virt")),
        P(("blk", "virt"), None),
        P(("blk", "virt")),
        P(),
        P(),
        P(),
    )
    return jax.shard_map(
        functools.partial(body, mesh.shape["blk"], mesh.shape["virt"]),
        mesh=mesh,
        in_specs=placed,
        out_specs=P(("blk", "virt"), None),
        check_vma=False,
    )
```

```python
import functools

import jax
import jax.numpy as jnp
from jax import lax
from jax.experimental import pallas as pl
from jax.experimental.pallas import tpu as pltpu
from jax.sharding import PartitionSpec as P

MESH = pl.DeviceIdType.MESH


def flip(index, bits):
    step = 1
    while step <= bits:
        if bits & step:
            index = index + step * (1 - 2 * ((index // step) % 2))
        step *= 2
    return index


def kernel(
    blk_count,
    virt_count,
    tiles_hbm,
    amp_hbm,
    readers_hbm,
    slots_hbm,
    mask_hbm,
    virt_hbm,
    occ_hbm,
    first_hbm,
    second_hbm,
    out_ref,
    tiles,
    amp,
    products,
    weights,
    partial,
    swapped,
    landed,
    denominator,
    hot,
    readers,
    slots,
    mask,
    virt_energy,
    occ,
    first,
    second,
    local_sem,
    z_send,
    z_recv,
    n_send,
    n_recv,
    sum_send,
    sum_recv,
):
    b = lax.axis_index("blk")
    v = lax.axis_index("virt")
    core = v % 2
    chip = v // 2
    kind = ((chip % 2) + ((chip // 2) % 2)) % 2
    generated = readers.shape[0]
    tile_rows = tiles.shape[0] // generated
    panel_rows, width = amp_hbm.shape
    rows = out_ref.shape[0]
    row_blocks = rows // tile_rows
    pairs = blk_count // 2

    locals_ = [
        pltpu.make_async_copy(source, target, local_sem.at[index])
        for index, (source, target) in enumerate(
            (
                (readers_hbm, readers),
                (slots_hbm, slots),
                (mask_hbm, mask),
                (virt_hbm, virt_energy),
                (occ_hbm, occ),
                (first_hbm, first),
                (second_hbm, second),
                (amp_hbm, amp.at[pl.ds(b * panel_rows, panel_rows)]),
                (tiles_hbm, tiles),
            )
        )
    ]

    barrier = pltpu.get_barrier_semaphore()
    for d in range(1, blk_count):
        pl.semaphore_signal(barrier, inc=1, device_id=(flip(b, d), v), device_id_type=MESH)
    for d in range(1, virt_count):
        pl.semaphore_signal(barrier, inc=1, device_id=(b, flip(v, d)), device_id_type=MESH)
    for copy in locals_:
        copy.start()
    pl.semaphore_wait(barrier, blk_count + virt_count - 2)

    half, piece = width // 2, width // 8
    spot = chip % 4

    def columns(core_now, spot_now):
        return pl.multiple_of(core_now * half + spot_now * piece, piece)

    def panel(d):
        return pl.ds(pl.multiple_of(flip(b, d) * panel_rows, panel_rows), panel_rows)

    mine = columns(core, spot)
    beside_x = columns(core, flip(spot, 1))
    beside_y = columns(core, flip(spot, 2))
    opposite = columns(core, flip(spot, 3))

    z_copies = {}
    for d in tuple(range(2, blk_count)) + (1,):
        copy = pltpu.make_async_remote_copy(
            amp_hbm.at[:, pl.ds(mine, piece)],
            amp.at[panel(0), pl.ds(mine, piece)],
            z_send.at[d],
            z_recv.at[d],
            device_id=(flip(b, d), v),
            device_id_type=MESH,
        )
        copy.start()
        z_copies[d] = copy

    n_copies = {}

    def share(d, which, start, size, bits):
        area = amp.at[panel(d), pl.ds(start, size)]
        copy = pltpu.make_async_remote_copy(
            area,
            area,
            n_send.at[d, which],
            n_recv.at[d, which],
            device_id=(b, flip(v, bits)),
            device_id_type=MESH,
        )
        copy.start()
        n_copies[d, which] = copy

    def spread(d):
        z_copies[d].wait_recv()
        share(d, 0, mine, piece, 2)
        share(d, 1, mine, piece, 4)
        if d == 1:
            share(d, 3, mine, piece, 6)
        share(d, 2, mine, piece, 1)

    def relay(d):
        n_copies[d, 0].wait_recv()
        if not d == 1:
            share(d, 3, beside_x, piece // 2, 4)
        n_copies[d, 1].wait_recv()
        if not d == 1:
            share(d, 4, pl.multiple_of(beside_y + piece // 2, piece // 2), piece // 2, 2)
        share(d, 5, beside_x, piece, 1)
        share(d, 6, beside_y, piece, 1)

    def finish(d):
        n_copies[d, 3].wait_recv()
        if not d == 1:
            n_copies[d, 4].wait_recv()
        share(d, 7, opposite, piece, 1)

    def settle(which, *panels):
        for d in panels:
            n_copies[d, which].wait_recv()

    for copy in locals_[:7]:
        copy.wait()
    chips = virt_count // 2
    all_rows = virt_count * rows
    core_rows = chips * rows
    lanes = generated * tile_rows
    lane = lax.broadcasted_iota(jnp.int32, (1, lanes), 1)
    goal = jnp.zeros((1, lanes), jnp.int32)
    for t in range(generated):
        place = (readers[t] % 2) * chips + readers[t] // 2
        goal = jnp.where(lane // tile_rows == t, (place * row_blocks + slots[t]) * tile_rows, goal)
    goal = goal + lane % tile_rows
    row = lax.broadcasted_iota(jnp.int32, (all_rows, lanes), 0)
    hot[...] = (row == goal).astype(jnp.float32).astype(jnp.bfloat16)

    levels = occ.shape[0]
    occ_row = occ[...].reshape(1, levels)
    occ_high = occ_row.astype(jnp.bfloat16).astype(jnp.float32)
    occ_rest = occ_row - occ_high
    occ_mid = occ_rest.astype(jnp.bfloat16).astype(jnp.float32)
    occ_low = occ_rest - occ_mid
    term = lax.broadcasted_iota(jnp.int32, (8, levels), 0)
    occ_terms = jnp.where(
        term == 0, occ_high, jnp.where(term == 1, occ_mid, jnp.where(term == 2, occ_low, 0.0))
    ).astype(jnp.bfloat16)
    count = first.shape[1]
    level = lax.broadcasted_iota(jnp.int32, (levels, count), 0)

    def energy(pair_ref):
        chosen = (level == pair_ref[...]).astype(jnp.float32).astype(jnp.bfloat16)
        terms = jnp.dot(occ_terms, chosen, preferred_element_type=jnp.float32)
        return (terms[0:1] + terms[1:2]) + terms[2:3]

    diagonal = lax.broadcasted_iota(jnp.int32, (rows, rows), 0) == lax.broadcasted_iota(
        jnp.int32, (rows, rows), 1
    )
    virt_column = jnp.sum(jnp.where(diagonal, virt_energy[...], 0.0), axis=1, keepdims=True)
    denominator[...] = (virt_column - energy(first)) - energy(second)

    sums = {}
    pair_width = 2 * panel_rows
    pair_lane = lax.broadcasted_iota(jnp.int32, (1, pair_width), 1)

    def multiply(i, spot_now, begin=False):
        rows_now = pl.ds(pl.multiple_of(flip(b // 2, i) * pair_width, pair_width), pair_width)
        total = None if begin else products[i]
        for core_now in range(2):
            depth = pl.ds(columns(core_now, spot_now), piece)
            term = lax.dot_general(
                tiles[:, depth],
                amp[rows_now, depth],
                (((1,), (1,)), ((), ())),
                preferred_element_type=jnp.float32,
            )
            total = term if total is None else total + term
        products[i] = total

    for i in range(pairs):
        g = flip(b // 2, i)
        weights[i] = jnp.concatenate(
            [
                jnp.broadcast_to(
                    jnp.where(pair_lane < panel_rows, mask[2 * g, t], mask[2 * g + 1, t]).astype(
                        jnp.float32
                    ),
                    (tile_rows, pair_width),
                )
                for t in range(generated)
            ],
            axis=0,
        )

    def contract(i):
        product = products[i]
        product = product * weights[i]
        high = product.astype(jnp.bfloat16)
        low = (product - high.astype(jnp.float32)).astype(jnp.bfloat16)
        terms = jnp.concatenate([high, low], axis=1)

        def gather_rows(core_now):
            area = pl.ds(pl.multiple_of(core_now * core_rows, core_rows), core_rows)
            both = jnp.dot(hot[area, :], terms, preferred_element_type=jnp.float32)
            partial[i, area, :] = both[:, :pair_width] + both[:, pair_width:]

        gather_rows(1 - core)
        copy = pltpu.make_async_remote_copy(
            partial.at[i, pl.ds(pl.multiple_of((1 - core) * core_rows, core_rows), core_rows)],
            swapped.at[i],
            sum_send.at[i, 0],
            sum_recv.at[i, 0],
            device_id=(b, flip(v, 1)),
            device_id_type=MESH,
        )
        copy.start()
        sums[i, 0] = copy
        gather_rows(core)

    def scatter(i):
        sums[i, 0].wait_recv()
        for d in (3, 1, 2) + tuple(range(4, chips)) + (0,):
            peer = flip(chip, d)
            area = pl.ds(pl.multiple_of(peer * rows, rows), rows)
            own = pl.ds(pl.multiple_of(core * core_rows + peer * rows, rows), rows)
            swapped[i, area, :] = swapped[i, area, :] + partial[i, own, :]
            if d == 0:
                continue
            copy = pltpu.make_async_remote_copy(
                swapped.at[i, area],
                landed.at[i, d],
                sum_send.at[i, d],
                sum_recv.at[i, d],
                device_id=(b, flip(v, 2 * d)),
                device_id_type=MESH,
            )
            copy.start()
            sums[i, d] = copy

    locals_[7].wait()
    locals_[8].wait()

    def gathered(i, step, *panels):
        settle((2, 5, 6, 7)[step], *panels)
        multiply(i, flip(spot, step), step == 0)

    for i in range(1, pairs):
        even, odd = 2 * i, 2 * i + 1
        if i == 1:
            spread(1)
        spread(even)
        spread(odd)
        if i == 1:
            relay(1)
            finish(1)
            for step in range(3):
                gathered(0, step, 1)
        relay(even)
        relay(odd)
        if i == 1:
            gathered(0, 3, 1)
            contract(0)
        for step in range(3):
            gathered(i, step, even, odd)
        finish(even)
        finish(odd)
        if i == 1:
            scatter(0)
        gathered(i, 3, even, odd)
        contract(i)
        scatter(i)

    for i in range(pairs):
        start = pl.multiple_of(flip(b // 2, i) * pair_width, pair_width)
        total = swapped[i, pl.ds(pl.multiple_of(chip * rows, rows), rows), :]
        for d in range(1, chips):
            sums[i, d].wait_recv()
            total = total + landed[i, d]
        out_ref[:, pl.ds(start, pair_width)] = (
            total / denominator[:, pl.ds(start, pair_width)]
        ).astype(out_ref.dtype)

    for copies in (z_copies, n_copies, sums):
        for copy in copies.values():
            copy.wait_send()


def body(
    blk_count,
    virt_count,
    integrals,
    amplitudes,
    readers,
    row_slots,
    tile_mask,
    virt_energy,
    occ_energy,
    pair_first,
    pair_second,
):
    generated, tile_rows, width = integrals.shape
    panel_rows = amplitudes.shape[0]
    rows = virt_energy.shape[0]
    columns = blk_count * panel_rows
    pairs = blk_count // 2
    levels = occ_energy.shape[0]
    anywhere = pl.BlockSpec(memory_space=pl.ANY)
    return pl.pallas_call(
        functools.partial(kernel, blk_count, virt_count),
        out_shape=jax.ShapeDtypeStruct((rows, columns), jnp.bfloat16),
        in_specs=[anywhere] * 9,
        out_specs=pl.BlockSpec(memory_space=pltpu.VMEM),
        scratch_shapes=[
            pltpu.VMEM((generated * tile_rows, width), jnp.bfloat16),
            pltpu.VMEM((columns, width), jnp.bfloat16),
            pltpu.VMEM((pairs, generated * tile_rows, 2 * panel_rows), jnp.float32),
            pltpu.VMEM((pairs, generated * tile_rows, 2 * panel_rows), jnp.float32),
            pltpu.VMEM((pairs, virt_count * rows, 2 * panel_rows), jnp.float32),
            pltpu.VMEM((pairs, virt_count // 2 * rows, 2 * panel_rows), jnp.float32),
            pltpu.VMEM((pairs, virt_count // 2, rows, 2 * panel_rows), jnp.float32),
            pltpu.VMEM((rows, columns), jnp.float32),
            pltpu.VMEM((virt_count * rows, generated * tile_rows), jnp.bfloat16),
            pltpu.SMEM((generated,), jnp.int32),
            pltpu.SMEM((generated,), jnp.int32),
            pltpu.SMEM((blk_count, generated), jnp.int32),
            pltpu.VMEM((1, rows), jnp.float32),
            pltpu.VMEM((levels,), jnp.float32),
            pltpu.VMEM((1, columns), jnp.int32),
            pltpu.VMEM((1, columns), jnp.int32),
            pltpu.SemaphoreType.DMA((9,)),
            pltpu.SemaphoreType.DMA((blk_count,)),
            pltpu.SemaphoreType.DMA((blk_count,)),
            pltpu.SemaphoreType.DMA((blk_count, 8)),
            pltpu.SemaphoreType.DMA((blk_count, 8)),
            pltpu.SemaphoreType.DMA((pairs, virt_count // 2)),
            pltpu.SemaphoreType.DMA((pairs, virt_count // 2)),
        ],
        compiler_params=pltpu.CompilerParams(
            collective_id=0, has_side_effects=True, vmem_limit_bytes=60 * 1024 * 1024
        ),
        name="ladder",
    )(
        integrals.reshape(generated * tile_rows, width),
        amplitudes,
        readers,
        row_slots,
        tile_mask.T,
        virt_energy.reshape(1, rows),
        occ_energy,
        pair_first.reshape(1, columns),
        pair_second.reshape(1, columns),
    )


def solution(mesh):
    placed = (
        P(("blk", "virt"), None, None),
        P("blk", None),
        P(("blk", "virt")),
        P(("blk", "virt")),
        P(("blk", "virt"), None),
        P(("blk", "virt")),
        P(),
        P(),
        P(),
    )
    return jax.shard_map(
        functools.partial(body, mesh.shape["blk"], mesh.shape["virt"]),
        mesh=mesh,
        in_specs=placed,
        out_specs=P(("blk", "virt"), None),
        check_vma=False,
    )
```
